32 devices in a mesh: seq: 8 (over y, x, core), head: 4 (over z).
Axes of the slice: x: 2, y: 2, z: 4, core: 2. Of those that a mesh axis runs over, the one named last changes fastest.
Arguments:
- incoming_hidden: bfloat16 [8192, 1024], P(('seq', 'head')), may hold values from -6 to 6
- earliest_block_vals: bfloat16 [8192, 1024], P('seq', 'head'), may hold values from -6 to 6
- upstream_sensitivity: bfloat16 [8192, 1024], P(('seq', 'head')), may hold values from -6 to 6
- opening_standardize_factor: float32 [1024], replicated, may hold values from 0.5 to 1.5
- opening_standardize_shift: float32 [1024], replicated, may hold values from -1.5 to 1.5
- attention_lag_blend: float32 [6, 1024], replicated, may hold values from 0 to 1
- acceptor_linear_map: bfloat16 [1024, 1024], P('seq', 'head'), may hold values from -0.1875 to 0.1875
- address_linear_map: bfloat16 [1024, 1024], P('seq', 'head'), may hold values from -0.1875 to 0.1875
- content_linear_map: bfloat16 [1024, 1024], P('seq', 'head'), may hold values from -0.1875 to 0.1875
- fading_narrowing: bfloat16 [1024, 64], P('seq'), may hold values from -0.1875 to 0.1875
- fading_widening: bfloat16 [64, 1024], P('seq', 'head'), may hold values from -0.75 to 0.75
- fading_baseline: float32 [1024], P('head'), may hold values from -12 to -1
- stepsize_narrowing: bfloat16 [1024, 64], P('seq'), may hold values from -0.1875 to 0.1875
- stepsize_widening: bfloat16 [64, 1024], P('seq', 'head'), may hold values from -0.75 to 0.75
- stepsize_baseline: float32 [1024], P('head'), may hold values from -10 to 1
- residual_blend_narrowing: bfloat16 [1024, 32], P('seq'), may hold values from -0.1875 to 0.1875
- residual_blend_widening: bfloat16 [32, 1024], P('seq', 'head'), may hold values from -1 to 1
- residual_blend_baseline: float32 [1024], P('head'), may hold values from -4 to 4
- valve_narrowing: bfloat16 [1024, 128], P('seq'), may hold values from -0.1875 to 0.1875
- valve_widening: bfloat16 [128, 1024], P('seq', 'head'), may hold values from -0.5 to 0.5
- erasing_address_factor: float32 [1024], P('head'), may hold values from 0.3 to 3
- address_rate_portion: float32 [1024], P('head'), may hold values from 0 to 1
- present_extra_factor: float32 [1024], P('head'), may hold values from -1 to 1
- attend_standardize_factor: float32 [1024], P('head'), may hold values from 0.25 to 1.75
- attend_standardize_shift: float32 [1024], P('head'), may hold values from -1.5 to 1.5
- emitted_linear_map: bfloat16 [1024, 1024], P('head', 'seq'), may hold values from -0.1875 to 0.1875
- closing_standardize_factor: float32 [1024], replicated, may hold values from 0.5 to 1.5
- closing_standardize_shift: float32 [1024], replicated, may hold values from -1.5 to 1.5
- feedforward_lag_blend: float32 [1024], replicated, may hold values from 0 to 1
- feedforward_entrance: bfloat16 [1024, 4096], P('seq', 'head'), may hold values from -0.1875 to 0.1875
- feedforward_exit: bfloat16 [4096, 1024], P('head', 'seq'), may hold values from -0.09375 to 0.09375
Outputs:
- hidden_out: bfloat16 [8192, 1024], P(('seq', 'head'))
- incoming_hidden_adjoint: float32 [8192, 1024], P(('seq', 'head'))
- earliest_block_vals_adjoint: float32 [8192, 1024], P('seq', 'head')
- opening_standardize_factor_adj: float32 [1024], replicated
- opening_standardize_shift_adj: float32 [1024], replicated
- attention_lag_blend_adjoint: float32 [5, 1024], replicated
- decay_lag_blend_adjoint: float32 [1024], replicated
- acceptor_linear_map_adjoint: float32 [1024, 1024], P('seq', 'head')
- address_linear_map_adjoint: float32 [1024, 1024], P('seq', 'head')
- content_linear_map_adjoint: float32 [1024, 1024], P('seq', 'head')
- fading_narrowing_adjoint: float32 [1024, 64], P('seq')
- fading_widening_adjoint: float32 [64, 1024], P('seq', 'head')
- fading_baseline_adjoint: float32 [1024], P('head')
- stepsize_narrowing_adjoint: float32 [1024, 64], P('seq')
- stepsize_widening_adjoint: float32 [64, 1024], P('seq', 'head')
- stepsize_baseline_adjoint: float32 [1024], P('head')
- residual_blend_narrowing_adj: float32 [1024, 32], P('seq')
- residual_blend_widening_adj: float32 [32, 1024], P('seq', 'head')
- residual_blend_baseline_adj: float32 [1024], P('head')
- valve_narrowing_adjoint: float32 [1024, 128], P('seq')
- valve_widening_adjoint: float32 [128, 1024], P('seq', 'head')
- erasing_address_factor_adj: float32 [1024], P('head')
- address_rate_portion_adjoint: float32 [1024], P('head')
- present_extra_adjoint: float32 [1024], P('head')
- attend_standardize_factor_adj: float32 [1024], P('head')
- attend_standardize_shift_adj: float32 [1024], P('head')
- emitted_linear_map_adjoint: float32 [1024, 1024], P('head', 'seq')
- closing_standardize_factor_adj: float32 [1024], replicated
- closing_standardize_shift_adj: float32 [1024], replicated
- feedforward_lag_blend_adjoint: float32 [1024], replicated
- feedforward_entrance_adjoint: float32 [1024, 4096], P('seq', 'head')
- feedforward_exit_adjoint: float32 [4096, 1024], P('head', 'seq')
The draws below stay inside these ranges and needn't reach their ends.
All inputs are finite; a program needn't handle non-finite values.
Results may differ from the reference program's by a relative error of at most 0.028.
Values may be sent and summed in bfloat16 or wider, within the bound.
No kernel may reach another device: no remote copies, remote signals or barrier semaphores. Data moves between devices by JAX's collectives and lax.ppermute only.
A program may use at most 256 MiB of HBM per device.

```python
import math
import jax
import jax.numpy as jnp
from jax import lax

HEADS = 16
ATTEND_FEATURES = 64
EMBED_SIZE = 1024
FF = 4096
DECAY_RANK = 64
RATE_RANK = 64
BLEND_RANK = 32
GATE_RANK = 128
BLOCK = 64
TOKENS = 8192


def slow_heads(key):
    order = jax.random.permutation(jax.random.fold_in(key, 17), HEADS)
    return (order < HEADS // 2)[:, None]


def two_ranges(key, salt, slow_low, slow_high, fast_low, fast_high):
    slow_values = jax.random.uniform(jax.random.fold_in(key, salt), (HEADS, ATTEND_FEATURES), jnp.float32, slow_low, slow_high)
    fast_values = jax.random.uniform(jax.random.fold_in(key, salt + 1), (HEADS, ATTEND_FEATURES), jnp.float32, fast_low, fast_high)
    return jnp.where(slow_heads(key), slow_values, fast_values).reshape(-1).astype(jnp.float32)


def draw_fading_baseline(key, part):
    return two_ranges(key, 3, -12.0, -10.0, -5.0, -1.0)


def draw_stepsize_baseline(key, part):
    return two_ranges(key, 7, -10.0, -8.0, -3.0, 1.0)


def steps_of(key, extent, cuts, low, high):
    loudness, own = 1.0, jax.random.fold_in(key, 6)
    for dim, shards_of in cuts:
        draws = jnp.exp(jax.random.uniform(jax.random.fold_in(own, dim), (shards_of,), jnp.float32, low / len(cuts), high / len(cuts)))
        loudness = loudness * jnp.repeat(draws, extent[dim] // shards_of).reshape([-1 if axis == dim else 1 for axis in range(len(extent))])
    return loudness


def gaussian(rng, dims, deviation, limit, split=(), held_as=jnp.bfloat16):
    values = jax.random.normal(rng, dims, jnp.float32) * deviation
    if len(split) > 0:
        values = steps_of(rng, dims, split, -0.22, 0.18) * values
    return jnp.clip(values, min=-limit, max=limit).astype(held_as)


def setup_inputs(seed: int = 0) -> dict:
    seeds = jax.random.split(jax.random.key(seed), 32)
    incoming_hidden = gaussian(seeds[0], (TOKENS, EMBED_SIZE), 1.0, 6.0, ((0, 32),))
    earliest_block_vals = gaussian(seeds[1], (TOKENS, EMBED_SIZE), 1.0, 6.0, ((0, 8), (1, 4)))
    upstream_sensitivity = gaussian(seeds[2], (TOKENS, EMBED_SIZE), 1.0, 6.0, ((0, 32),))
    opening_standardize_factor = jnp.clip(1.0 + 0.1 * jax.random.normal(seeds[3], (EMBED_SIZE,), jnp.float32), 0.5, 1.5)
    opening_standardize_shift = gaussian(seeds[4], (EMBED_SIZE,), 0.3, 1.5, (), jnp.float32)
    attention_lag_blend = jnp.clip(jax.random.uniform(seeds[5], (6, EMBED_SIZE), jnp.float32, 0.0, 1.0), 0.0, 1.0)
    acceptor_linear_map = gaussian(seeds[6], (EMBED_SIZE, EMBED_SIZE), EMBED_SIZE ** -0.5, 0.1875, ((0, 8), (1, 4)))
    address_linear_map = gaussian(seeds[7], (EMBED_SIZE, EMBED_SIZE), EMBED_SIZE ** -0.5, 0.1875, ((0, 8), (1, 4)))
    content_linear_map = gaussian(seeds[8], (EMBED_SIZE, EMBED_SIZE), EMBED_SIZE ** -0.5, 0.1875, ((0, 8), (1, 4)))
    fading_narrowing = gaussian(seeds[9], (EMBED_SIZE, DECAY_RANK), EMBED_SIZE ** -0.5, 0.1875, ((0, 8),))
    fading_widening = gaussian(seeds[10], (DECAY_RANK, EMBED_SIZE), DECAY_RANK ** -0.5, 0.75, ((0, 8), (1, 4)))
    fading_baseline = draw_fading_baseline(jax.random.fold_in(seeds[31], 71), 0)
    stepsize_narrowing = gaussian(seeds[12], (EMBED_SIZE, RATE_RANK), EMBED_SIZE ** -0.5, 0.1875, ((0, 8),))
    stepsize_widening = gaussian(seeds[13], (RATE_RANK, EMBED_SIZE), RATE_RANK ** -0.5, 0.75, ((0, 8), (1, 4)))
    stepsize_baseline = draw_stepsize_baseline(jax.random.fold_in(seeds[31], 71), 0)
    residual_blend_narrowing = gaussian(seeds[15], (EMBED_SIZE, BLEND_RANK), EMBED_SIZE ** -0.5, 0.1875, ((0, 8),))
    residual_blend_widening = gaussian(seeds[16], (BLEND_RANK, EMBED_SIZE), BLEND_RANK ** -0.5, 1.0, ((0, 8), (1, 4)))
    residual_blend_baseline = gaussian(seeds[17], (EMBED_SIZE,), 1.0, 4.0, ((0, 4),), jnp.float32)
    valve_narrowing = gaussian(seeds[18], (EMBED_SIZE, GATE_RANK), EMBED_SIZE ** -0.5, 0.1875, ((0, 8),))
    valve_widening = gaussian(seeds[19], (GATE_RANK, EMBED_SIZE), GATE_RANK ** -0.5, 0.5, ((0, 8), (1, 4)))
    erasing_address_factor = jnp.clip(jnp.exp(math.log(3.0) - 2.3025851 * jax.random.uniform(seeds[20], (EMBED_SIZE,), jnp.float32) ** steps_of(seeds[20], (EMBED_SIZE,), ((0, 4),), -0.2, 0.2)), 0.3, 3.0)
    address_rate_portion = jnp.clip(1.0 * jax.random.uniform(seeds[21], (EMBED_SIZE,), jnp.float32) ** steps_of(seeds[21], (EMBED_SIZE,), ((0, 4),), -0.2, 0.2), 0.0, 1.0)
    present_extra_factor = gaussian(seeds[22], (EMBED_SIZE,), 0.2, 1.0, ((0, 4),), jnp.float32)
    attend_standardize_factor = jnp.clip(1.0 + 0.15 * jax.random.normal(seeds[23], (EMBED_SIZE,), jnp.float32), 0.25, 1.75)
    attend_standardize_shift = gaussian(seeds[24], (EMBED_SIZE,), 0.3, 1.5, ((0, 4),), jnp.float32)
    emitted_linear_map = gaussian(seeds[25], (EMBED_SIZE, EMBED_SIZE), EMBED_SIZE ** -0.5, 0.1875, ((0, 4), (1, 8)))
    closing_standardize_factor = jnp.clip(1.0 + 0.1 * jax.random.normal(seeds[26], (EMBED_SIZE,), jnp.float32), 0.5, 1.5)
    closing_standardize_shift = gaussian(seeds[27], (EMBED_SIZE,), 0.3, 1.5, (), jnp.float32)
    feedforward_lag_blend = jnp.clip(jax.random.uniform(seeds[28], (EMBED_SIZE,), jnp.float32, 0.0, 1.0), 0.0, 1.0)
    feedforward_entrance = gaussian(seeds[29], (EMBED_SIZE, FF), EMBED_SIZE ** -0.5, 0.1875, ((0, 8), (1, 4)))
    feedforward_exit = gaussian(seeds[30], (FF, EMBED_SIZE), FF ** -0.5, 0.09375, ((0, 4), (1, 8)))
    return {"incoming_hidden": incoming_hidden, "earliest_block_vals": earliest_block_vals, "upstream_sensitivity": upstream_sensitivity, "opening_standardize_factor": opening_standardize_factor, "opening_standardize_shift": opening_standardize_shift, "attention_lag_blend": attention_lag_blend, "acceptor_linear_map": acceptor_linear_map, "address_linear_map": address_linear_map, "content_linear_map": content_linear_map, "fading_narrowing": fading_narrowing, "fading_widening": fading_widening, "fading_baseline": fading_baseline, "stepsize_narrowing": stepsize_narrowing, "stepsize_widening": stepsize_widening, "stepsize_baseline": stepsize_baseline, "residual_blend_narrowing": residual_blend_narrowing, "residual_blend_widening": residual_blend_widening, "residual_blend_baseline": residual_blend_baseline, "valve_narrowing": valve_narrowing, "valve_widening": valve_widening, "erasing_address_factor": erasing_address_factor, "address_rate_portion": address_rate_portion, "present_extra_factor": present_extra_factor, "attend_standardize_factor": attend_standardize_factor, "attend_standardize_shift": attend_standardize_shift, "emitted_linear_map": emitted_linear_map, "closing_standardize_factor": closing_standardize_factor, "closing_standardize_shift": closing_standardize_shift, "feedforward_lag_blend": feedforward_lag_blend, "feedforward_entrance": feedforward_entrance, "feedforward_exit": feedforward_exit}


@jax.custom_vjp
def narrow_bottleneck(v):
    return lax.optimization_barrier(v.astype(jnp.bfloat16)).astype(jnp.float32)

@jax.custom_vjp
def low_back(v):
    return v

def low_keep(v):
    return (narrow_bottleneck(v), None)

def low_pass(kept, grad):
    return (grad,)

def back_keep(v):
    return (v, None)

def back_low(kept, grad):
    return (narrow_bottleneck(grad),)
narrow_bottleneck.defvjp(low_keep, low_pass)
low_back.defvjp(back_keep, back_low)

def matmul(left, right):
    return jnp.dot(left, right, precision=lax.Precision.HIGHEST, preferred_element_type=jnp.float32)

def layer_norm(content_tokens, norm_gain, norm_bias):
    row_mean = lax.optimization_barrier(jnp.mean(content_tokens, axis=-1, keepdims=True))
    centred = content_tokens - row_mean
    row_var = lax.optimization_barrier(jnp.mean(centred * centred, axis=-1, keepdims=True))
    return centred * lax.rsqrt(row_var + 1e-05) * norm_gain + norm_bias

def shift_rows(content_tokens):
    return jnp.concatenate([jnp.zeros_like(content_tokens[:1]), content_tokens[:-1]], axis=0)

def prepare(acceptor_tokens, key_base, value_base, decay_prod, rate_prod, blend_prod, earliest_block_vals, fading_baseline, stepsize_baseline, residual_blend_baseline, erasing_address_factor, address_rate_portion):
    token_total = acceptor_tokens.shape[0]
    log_decay = -jnp.exp(-jax.nn.softplus(-(fading_baseline + decay_prod)) - 0.5)
    rate_vals = jax.nn.sigmoid(stepsize_baseline + rate_prod)
    blend_vals = jax.nn.sigmoid(residual_blend_baseline + blend_prod)
    content_tokens = value_base + (earliest_block_vals - value_base) * blend_vals
    removal = (key_base * erasing_address_factor).reshape(token_total, -1, ATTEND_FEATURES)
    removal = removal * lax.rsqrt(lax.optimization_barrier(jnp.sum(removal * removal, axis=-1, keepdims=True)) + 1e-06)
    address_signals = key_base * (1.0 + (rate_vals - 1.0) * address_rate_portion)
    return (acceptor_tokens.reshape(token_total, -1, ATTEND_FEATURES), log_decay.reshape(token_total, -1, ATTEND_FEATURES), removal, rate_vals.reshape(token_total, -1, ATTEND_FEATURES), address_signals.reshape(token_total, -1, ATTEND_FEATURES), content_tokens.reshape(token_total, -1, ATTEND_FEATURES))

def wrap_around_rule(emitted_tokens, acceptor_tokens, address_signals, content_tokens, sigmoid_valve_levels, present_extra_factor, attend_standardize_factor, attend_standardize_shift):
    token_total = emitted_tokens.shape[0]
    head_mean = lax.optimization_barrier(jnp.mean(emitted_tokens, axis=-1, keepdims=True))
    centred = emitted_tokens - head_mean
    head_var = lax.optimization_barrier(jnp.mean(centred * centred, axis=-1, keepdims=True))
    per_attend_split = (centred * lax.rsqrt(head_var + 0.00064)).reshape(token_total, -1) * attend_standardize_factor + attend_standardize_shift
    present_token_extra = lax.optimization_barrier(jnp.sum(acceptor_tokens * address_signals * present_extra_factor.reshape(-1, ATTEND_FEATURES), axis=-1, keepdims=True)) * content_tokens
    return (per_attend_split + present_token_extra.reshape(token_total, -1)) * sigmoid_valve_levels

def delta_block(carried, block):

    def one_token(state, token_in):
        acceptor_tokens, log_decay, removal, rate_vals, address_signals, content_tokens = token_in
        pulled = jnp.einsum('hij,hj->hi', state, -removal, precision=lax.Precision.HIGHEST)
        state = state * jnp.exp(log_decay)[:, None, :] + pulled[:, :, None] * (removal * rate_vals)[:, None, :] + content_tokens[:, :, None] * address_signals[:, None, :]
        output = jnp.einsum('hij,hj->hi', state, acceptor_tokens, precision=lax.Precision.HIGHEST)
        return (state, output)
    return lax.scan(one_token, carried, block)

def delta_rule(acceptor_tokens, log_decay, removal, rate_vals, address_signals, content_tokens):
    blocks = tuple((component_element.reshape(-1, BLOCK, HEADS, ATTEND_FEATURES) for component_element in (acceptor_tokens, log_decay, removal, rate_vals, address_signals, content_tokens)))
    start = jnp.zeros((HEADS, ATTEND_FEATURES, ATTEND_FEATURES), jnp.float32)
    last_state, emitted_tokens = lax.scan(jax.checkpoint(delta_block), start, blocks)
    return emitted_tokens.reshape(-1, HEADS, ATTEND_FEATURES)

def evaluate_layerwise(incoming_hidden, earliest_block_vals, opening_standardize_factor, opening_standardize_shift, attention_lag_blend, acceptor_linear_map, address_linear_map, content_linear_map, fading_narrowing, fading_widening, fading_baseline, stepsize_narrowing, stepsize_widening, stepsize_baseline, residual_blend_narrowing, residual_blend_widening, residual_blend_baseline, valve_narrowing, valve_widening, erasing_address_factor, address_rate_portion, present_extra_factor, attend_standardize_factor, attend_standardize_shift, emitted_linear_map, closing_standardize_factor, closing_standardize_shift, feedforward_lag_blend, feedforward_entrance, feedforward_exit):
    normed = narrow_bottleneck(layer_norm(incoming_hidden, opening_standardize_factor, opening_standardize_shift))
    shift_delta = shift_rows(normed) - normed
    mixed_in = [narrow_bottleneck(normed + shift_delta * attention_lag_blend[position]) for position in range(6)]
    acceptor_tokens = low_back(matmul(mixed_in[0], acceptor_linear_map))
    decay_prod = low_back(matmul(narrow_bottleneck(jnp.tanh(low_back(matmul(mixed_in[1], fading_narrowing)))), fading_widening))
    key_base = low_back(matmul(mixed_in[2], address_linear_map))
    value_base = low_back(matmul(mixed_in[3], content_linear_map))
    blend_prod = low_back(matmul(narrow_bottleneck(low_back(matmul(mixed_in[3], residual_blend_narrowing))), residual_blend_widening))
    rate_prod = low_back(matmul(narrow_bottleneck(low_back(matmul(mixed_in[4], stepsize_narrowing))), stepsize_widening))
    sigmoid_valve_levels = low_back(matmul(narrow_bottleneck(jax.nn.sigmoid(low_back(matmul(mixed_in[5], valve_narrowing)))), valve_widening))
    scan_operands = prepare(acceptor_tokens, key_base, value_base, decay_prod, rate_prod, blend_prod, earliest_block_vals, fading_baseline, stepsize_baseline, residual_blend_baseline, erasing_address_factor, address_rate_portion)
    emitted_tokens = delta_rule(*scan_operands)
    auxiliary_path = narrow_bottleneck(wrap_around_rule(emitted_tokens, scan_operands[0], scan_operands[4], scan_operands[5], sigmoid_valve_levels, present_extra_factor, attend_standardize_factor, attend_standardize_shift))
    middle = incoming_hidden + low_back(matmul(auxiliary_path, emitted_linear_map))
    normed_mid = narrow_bottleneck(layer_norm(middle, closing_standardize_factor, closing_standardize_shift))
    keyed_in = narrow_bottleneck(normed_mid + (shift_rows(normed_mid) - normed_mid) * feedforward_lag_blend)
    hidden = narrow_bottleneck(jnp.square(jax.nn.relu(low_back(matmul(keyed_in, feedforward_entrance)))))
    return middle + matmul(hidden, feedforward_exit)

def reference(incoming_hidden, earliest_block_vals, upstream_sensitivity, opening_standardize_factor, opening_standardize_shift, attention_lag_blend, acceptor_linear_map, address_linear_map, content_linear_map, fading_narrowing, fading_widening, fading_baseline, stepsize_narrowing, stepsize_widening, stepsize_baseline, residual_blend_narrowing, residual_blend_widening, residual_blend_baseline, valve_narrowing, valve_widening, erasing_address_factor, address_rate_portion, present_extra_factor, attend_standardize_factor, attend_standardize_shift, emitted_linear_map, closing_standardize_factor, closing_standardize_shift, feedforward_lag_blend, feedforward_entrance, feedforward_exit):
    real_numbers = [component_element.astype(jnp.float32) for component_element in (incoming_hidden, earliest_block_vals, opening_standardize_factor, opening_standardize_shift, attention_lag_blend, acceptor_linear_map, address_linear_map, content_linear_map, fading_narrowing, fading_widening, fading_baseline, stepsize_narrowing, stepsize_widening, stepsize_baseline, residual_blend_narrowing, residual_blend_widening, residual_blend_baseline, valve_narrowing, valve_widening, erasing_address_factor, address_rate_portion, present_extra_factor, attend_standardize_factor, attend_standardize_shift, emitted_linear_map, closing_standardize_factor, closing_standardize_shift, feedforward_lag_blend, feedforward_entrance, feedforward_exit)]
    evaluated_answer, reverse_sweep = jax.vjp(evaluate_layerwise, *real_numbers)
    incoming_hidden_adjoint, earliest_block_vals_adjoint, opening_standardize_factor_adj, opening_standardize_shift_adj, shift_sums, acceptor_linear_map_adjoint, address_linear_map_adjoint, content_linear_map_adjoint, fading_narrowing_adjoint, fading_widening_adjoint, fading_baseline_adjoint, stepsize_narrowing_adjoint, stepsize_widening_adjoint, stepsize_baseline_adjoint, residual_blend_narrowing_adj, residual_blend_widening_adj, residual_blend_baseline_adj, valve_narrowing_adjoint, valve_widening_adjoint, erasing_address_factor_adj, address_rate_portion_adjoint, present_extra_adjoint, attend_standardize_factor_adj, attend_standardize_shift_adj, emitted_linear_map_adjoint, closing_standardize_factor_adj, closing_standardize_shift_adj, feedforward_lag_blend_adjoint, feedforward_entrance_adjoint, feedforward_exit_adjoint = reverse_sweep(upstream_sensitivity.astype(jnp.float32))
    attention_lag_blend_adjoint = jnp.concatenate([shift_sums[:1], shift_sums[2:]], axis=0)
    decay_lag_blend_adjoint = shift_sums[1]
    return (evaluated_answer.astype(jnp.bfloat16), incoming_hidden_adjoint, earliest_block_vals_adjoint, opening_standardize_factor_adj, opening_standardize_shift_adj, attention_lag_blend_adjoint, decay_lag_blend_adjoint, acceptor_linear_map_adjoint, address_linear_map_adjoint, content_linear_map_adjoint, fading_narrowing_adjoint, fading_widening_adjoint, fading_baseline_adjoint, stepsize_narrowing_adjoint, stepsize_widening_adjoint, stepsize_baseline_adjoint, residual_blend_narrowing_adj, residual_blend_widening_adj, residual_blend_baseline_adj, valve_narrowing_adjoint, valve_widening_adjoint, erasing_address_factor_adj, address_rate_portion_adjoint, present_extra_adjoint, attend_standardize_factor_adj, attend_standardize_shift_adj, emitted_linear_map_adjoint, closing_standardize_factor_adj, closing_standardize_shift_adj, feedforward_lag_blend_adjoint, feedforward_entrance_adjoint, feedforward_exit_adjoint)
```

```python
import functools

import jax
import jax.numpy as jnp
from jax import lax
from jax.experimental import pallas as pl
from jax.experimental.pallas import tpu as pltpu
from jax.sharding import PartitionSpec as P

WIDTH = 64
BLOCK = 64
PAIR = 2 * WIDTH
HIGHEST = lax.Precision.HIGHEST
NN = (((1,), (0,)), ((), ()))
NT = (((1,), (1,)), ((), ()))
TN = (((0,), (0,)), ((), ()))
F32 = jnp.float32
BF16 = jnp.bfloat16
PASSES = 3
GROUP = 4


def mm(left, right, dims, passes=PASSES):
    left_high = left.astype(BF16)
    right_high = right.astype(BF16)

    def dot(a, b):
        return lax.dot_general(a, b, dims, preferred_element_type=F32)

    out = dot(left_high, right_high)
    if passes >= 2:
        out = out + dot((left - left_high.astype(F32)).astype(BF16), right_high)
    if passes >= 3:
        out = out + dot(left_high, (right - right_high.astype(F32)).astype(BF16))
    return out


def iotas(n):
    return lax.broadcasted_iota(jnp.int32, (n, n), 0), lax.broadcasted_iota(jnp.int32, (n, n), 1)


def stack_pair(x):
    lane = lax.broadcasted_iota(jnp.int32, x.shape, 1)
    return jnp.concatenate(
        [jnp.where(lane < WIDTH, x, 0.0), jnp.where(lane < WIDTH, 0.0, x)], axis=0
    )


def join_pair(x):
    half = x.shape[0] // 2
    return x[:half] + x[half:]


def running_sum(x, reverse=False):
    row, col = iotas(BLOCK)
    ones = jnp.where((row <= col) if reverse else (row >= col), 1.0, 0.0).astype(BF16)
    high = x.astype(BF16)
    rest = x - high.astype(F32)
    middle = rest.astype(BF16)
    low = (rest - middle.astype(F32)).astype(BF16)

    def dot(part):
        return lax.dot_general(ones, part, NN, preferred_element_type=F32)

    return dot(high) + dot(middle) + dot(low)


def factors(recept, log_decay, removal, rate, key):
    total = running_sum(log_decay)
    before = total - log_decay
    end = total[BLOCK - 1 : BLOCK]
    grow = jnp.exp(-total)
    fade = jnp.exp(end - total)
    decay = jnp.exp(total)
    decay_before = jnp.exp(before)
    write = removal * rate
    return dict(
        A=-removal * decay_before,
        B=write * grow,
        K=key * grow,
        R=recept * decay,
        BF=write * fade,
        KF=key * fade,
        decay=decay,
        decay_before=decay_before,
        grow=grow,
        fade=fade,
        end=jnp.exp(end),
        write=write,
    )


def causal_mask():
    row, col = iotas(2 * PAIR)
    same = ((row >> 6) & 1) == ((col >> 6) & 1)
    limit = jnp.where(row < PAIR, (row & 63) - 1, row & 63)
    return same & ((col & 63) <= limit)


def triangle_inverses(mats):
    row, col = iotas(PAIR)
    eye = jnp.where(row == col, 1.0, 0.0)
    outs = [eye + jnp.where((row >> 1) == (col >> 1), m, 0.0) for m in mats]
    for level in range(1, 6):
        pick = ((row >> (level + 1)) == (col >> (level + 1))) & ((row >> level) != (col >> level))
        steps = [mm(jnp.where(pick, m, 0.0), x, NN) for m, x in zip(mats, outs)]
        outs = [x + mm(x, s, NN) for x, s in zip(outs, steps)]
    return outs


def forward_kernel(
    group, recept, log_decay, removal, rate, key, val,
    query, local, pairs, inverse, pull, pulled, mapped, transfer, prefix, ending, carry,
):
    sides = recept.shape[1] // PAIR
    row, col = iotas(PAIR)
    eye = jnp.where(row == col, 1.0, 0.0)

    @pl.when(pl.program_id(0) == 0)
    def _():
        for p in range(sides):
            carry[p] = jnp.concatenate([eye, jnp.zeros((PAIR, PAIR), F32)], axis=0)

    mask = causal_mask()
    units = [(j, p) for j in range(group) for p in range(sides)]
    facs, scores, firsts = [], [], []
    for j, p in units:
        rows, lanes = slice(BLOCK * j, BLOCK * j + BLOCK), slice(PAIR * p, PAIR * p + PAIR)
        f = factors(
            recept[rows, lanes], log_decay[rows, lanes], removal[rows, lanes],
            rate[rows, lanes], key[rows, lanes],
        )
        f = {n: (v if n == "end" else stack_pair(v)) for n, v in f.items()
             if n in ("A", "B", "K", "R", "BF", "KF", "end")}
        f["V"] = stack_pair(val[rows, lanes])
        e = mm(
            jnp.concatenate([f["A"], f["R"]], axis=0), jnp.concatenate([f["B"], f["K"]], axis=0), NT
        )
        e = jnp.where(mask, e, 0.0)
        pairs[j, p] = e.astype(pairs.dtype)
        facs.append(f)
        scores.append(e)
        firsts.append(mm(e[:, PAIR:], f["V"], NN))
    inverses = triangle_inverses([e[:PAIR, :PAIR] for e in scores])
    wus = [
        mm(x, jnp.concatenate([f["A"], n[:PAIR]], axis=1), NN)
        for x, f, n in zip(inverses, facs, firsts)
    ]
    reads = [mm(e[PAIR:, :PAIR], wu, NN) for e, wu in zip(scores, wus)]
    writes = [mm(wu, f["BF"], TN) for wu, f in zip(wus, facs)]
    adds = [mm(f["V"], f["KF"], TN) for f in facs]
    state = [carry[p] for p in range(sides)]
    for (j, p), f, x, wu, n, read, wrote, add in zip(
        units, facs, inverses, wus, firsts, reads, writes, adds
    ):
        rows, lanes = slice(BLOCK * j, BLOCK * j + BLOCK), slice(PAIR * p, PAIR * p + PAIR)
        mapping = f["R"] + read[:, :PAIR]
        step = jnp.where(row == col, jnp.broadcast_to(f["end"], (PAIR, PAIR)), 0.0) + wrote[:PAIR]
        both = mm(mapping, state[p], NT)
        query[rows, lanes] = join_pair(both[:, :PAIR])
        local[rows, lanes] = join_pair(both[:, PAIR:] + read[:, PAIR:] + n[PAIR:])
        inverse[j, p] = x.astype(inverse.dtype)
        pull[j, p] = wu[:, :PAIR].astype(pull.dtype)
        pulled[j, p] = wu[:, PAIR:].astype(pulled.dtype)
        mapped[j, p] = mapping.astype(mapped.dtype)
        transfer[j, p] = step.astype(transfer.dtype)
        prefix[j, p] = state[p].astype(prefix.dtype)
        moved = mm(state[p], step, NN)
        state[p] = jnp.concatenate([moved[:PAIR], moved[PAIR:] + wrote[PAIR:] + add], axis=0)
    for p in range(sides):
        carry[p] = state[p]
        ending[p, 0] = join_pair(state[p][:PAIR])
        ending[p, 1] = join_pair(state[p][PAIR:])


def core_forward(recept, log_decay, removal, rate, key, val):
    tokens, wide = recept.shape
    sides = wide // PAIR
    blocks = tokens // BLOCK
    row_spec = pl.BlockSpec((GROUP * BLOCK, wide), lambda i: (i, 0))

    def spec(a, b):
        return pl.BlockSpec((GROUP, sides, a, b), lambda i: (i, 0, 0, 0))

    def kept(a, b):
        return jax.ShapeDtypeStruct((blocks, sides, a, b), F32)

    outs = pl.pallas_call(
        functools.partial(forward_kernel, GROUP),
        grid=(blocks // GROUP,),
        in_specs=[row_spec] * 6,
        out_specs=[row_spec, row_spec, spec(2 * PAIR, 2 * PAIR)]
        + [spec(PAIR, PAIR)] * 5
        + [spec(2 * PAIR, PAIR), pl.BlockSpec((sides, 2, WIDTH, PAIR), lambda i: (0, 0, 0, 0))],
        out_shape=[jax.ShapeDtypeStruct((tokens, wide), F32)] * 2
        + [kept(2 * PAIR, 2 * PAIR)]
        + [kept(PAIR, PAIR)] * 5
        + [kept(2 * PAIR, PAIR), jax.ShapeDtypeStruct((sides, 2, WIDTH, PAIR), F32)],
        scratch_shapes=[pltpu.VMEM((sides, 2 * PAIR, PAIR), F32)],
        cost_estimate=pl.CostEstimate(
            flops=blocks * 1000 * PAIR**3,
            bytes_accessed=blocks * PAIR * PAIR * 4 * 24,
            transcendentals=tokens * wide * 5,
        ),
        name="core_forward",
    )(recept, log_decay, removal, rate, key, val)
    return outs[0], outs[1], outs[2:9], outs[9]


def combine_kernel(position, gathered, query, local, emitted, entering):
    for p in range(query.shape[1] // PAIR):

        def step(s, state):
            return mm(state, stack_pair(gathered[s, p, 0].astype(F32)), NN) + stack_pair(
                gathered[s, p, 1].astype(F32)
            )

        state = lax.fori_loop(0, position[0], step, jnp.zeros((PAIR, PAIR), F32))
        entering[p] = join_pair(state)
        lanes = slice(PAIR * p, PAIR * p + PAIR)
        emitted[:, lanes] = mm(query[:, lanes], state, NT) + local[:, lanes]


def combine(position, gathered, query, local):
    vmem = pl.BlockSpec(memory_space=pltpu.VMEM)
    return pl.pallas_call(
        combine_kernel,
        in_specs=[pl.BlockSpec(memory_space=pltpu.SMEM), vmem, vmem, vmem],
        out_specs=[vmem, vmem],
        out_shape=[
            jax.ShapeDtypeStruct(query.shape, F32),
            jax.ShapeDtypeStruct((query.shape[1] // PAIR, WIDTH, PAIR), F32),
        ],
        cost_estimate=pl.CostEstimate(
            flops=16 * PAIR**3 * 40, bytes_accessed=query.size * 12, transcendentals=0
        ),
        name="core_combine",
    )(position, gathered, query, local)


def backward_kernel(
    group, position, gathered, grads, recept, log_decay, removal, rate, key, val, grad_out,
    pairs, inverse, pull, pulled, mapped, transfer, prefix, entering,
    out_recept, out_decay, out_removal, out_rate, out_key, out_val, carry,
):
    sides = recept.shape[1] // PAIR

    @pl.when(pl.program_id(0) == 0)
    def _():
        last = gathered.shape[0] - 1
        for p in range(sides):

            def step(s, state):
                return mm(state, stack_pair(gathered[last - s, p, 0].astype(F32)), NT) + stack_pair(
                    grads[last - s, p].astype(F32)
                )

            carry[p] = lax.fori_loop(0, last - position[0], step, jnp.zeros((PAIR, PAIR), F32))

    mask = causal_mask()
    states = [carry[p] for p in range(sides)]
    begin = [stack_pair(entering[p]) for p in range(sides)]
    for j in reversed(range(group)):
        for p in range(sides):
            rows, lanes = slice(BLOCK * j, BLOCK * j + BLOCK), slice(PAIR * p, PAIR * p + PAIR)
            key_in, rate_in, removal_in = key[rows, lanes], rate[rows, lanes], removal[rows, lanes]
            f = factors(recept[rows, lanes], log_decay[rows, lanes], removal_in, rate_in, key_in)
            a, b, k, r, bf, kf = (stack_pair(f[n]) for n in ("A", "B", "K", "R", "BF", "KF"))
            v, go = stack_pair(val[rows, lanes]), stack_pair(grad_out[rows, lanes])
            g = states[p]
            e = pairs[j, p].astype(F32)
            pre = prefix[j, p].astype(F32)
            state = mm(begin[p], pre[:PAIR], NN) + pre[PAIR:]
            u = mm(pull[j, p].astype(F32), state, NT) + pulled[j, p].astype(F32)
            through = mm(jnp.concatenate([bf, kf], axis=0), g, NT)
            grad_u = mm(e[PAIR:, :PAIR], go, TN) + through[:PAIR]
            z = mm(inverse[j, p].astype(F32), grad_u, TN)
            zo = jnp.concatenate([z, go], axis=0)
            uv = jnp.concatenate([u, v], axis=0)
            d = jnp.where(mask, mm(zo, uv, NT), 0.0)
            left = mm(d, jnp.concatenate([b, k], axis=0), NN) + mm(zo, state, NN)
            right = mm(d, jnp.concatenate([a, r], axis=0), TN)
            grad_v = mm(e[:, PAIR:], zo, TN) + through[PAIR:]
            out = mm(uv, g, NN)
            states[p] = mm(g, transfer[j, p].astype(F32), NT) + mm(
                go, mapped[j, p].astype(F32), TN
            )
            grad_a, grad_r = join_pair(left[:PAIR]), join_pair(left[PAIR:])
            grad_b, grad_k = join_pair(right[:PAIR]), join_pair(right[PAIR:])
            grad_bf, grad_kf = join_pair(out[:PAIR]), join_pair(out[PAIR:])
            to_write = f["grow"] * grad_b + f["fade"] * grad_bf
            to_key = f["grow"] * grad_k + f["fade"] * grad_kf
            to_end = jnp.sum(
                f["BF"] * grad_bf + f["KF"] * grad_kf, axis=0, keepdims=True
            ) + f["end"] * jnp.sum(state * g, axis=0, keepdims=True)
            to_before = f["A"] * grad_a
            to_sum = f["R"] * grad_r - f["write"] * to_write - key_in * to_key + to_before
            out_recept[rows, lanes] = f["decay"] * grad_r
            out_decay[rows, lanes] = running_sum(to_sum, True) - to_before + to_end
            out_removal[rows, lanes] = rate_in * to_write - f["decay_before"] * grad_a
            out_rate[rows, lanes] = removal_in * to_write
            out_key[rows, lanes] = to_key
            out_val[rows, lanes] = join_pair(grad_v)
    for p in range(sides):
        carry[p] = states[p]


def core_backward(position, gathered, grads, operands, grad_out, saved, entering):
    tokens, wide = grad_out.shape
    sides = wide // PAIR
    blocks = tokens // BLOCK
    group = 2
    steps = blocks // group
    row_spec = pl.BlockSpec((group * BLOCK, wide), lambda i: (steps - 1 - i, 0))

    def spec(kept):
        return pl.BlockSpec((group,) + kept.shape[1:], lambda i: (steps - 1 - i, 0, 0, 0))

    vmem = pl.BlockSpec(memory_space=pltpu.VMEM)
    return pl.pallas_call(
        functools.partial(backward_kernel, group),
        grid=(steps,),
        in_specs=[pl.BlockSpec(memory_space=pltpu.SMEM), vmem, vmem]
        + [row_spec] * 7
        + [spec(kept) for kept in saved]
        + [vmem],
        out_specs=[row_spec] * 6,
        out_shape=[jax.ShapeDtypeStruct((tokens, wide), F32)] * 6,
        scratch_shapes=[pltpu.VMEM((sides, PAIR, PAIR), F32)],
        cost_estimate=pl.CostEstimate(
            flops=blocks * 800 * PAIR**3,
            bytes_accessed=blocks * PAIR * PAIR * 4 * 30,
            transcendentals=tokens * wide * 5,
        ),
        name="core_backward",
    )(position, gathered, grads, *operands, grad_out, *saved, entering)


def shifted(block, axis, distance):
    devices = range(lax.axis_size(axis))
    route = [(i - distance, i) for i in devices if i - distance in devices]
    return lax.ppermute(block, axis, route)


def product(left, right):
    return jnp.dot(left, right, preferred_element_type=F32)


def cross_rows(left, right):
    return lax.dot_general(left, right, TN, preferred_element_type=F32)


def cross_cols(left, right):
    return lax.dot_general(left, right, NT, preferred_element_type=F32)


def layer_norm(content_tokens, norm_gain, norm_bias):
    row_mean = jnp.mean(content_tokens, axis=-1, keepdims=True)
    centred = content_tokens - row_mean
    row_var = jnp.mean(centred * centred, axis=-1, keepdims=True)
    return centred * lax.rsqrt(row_var + 1e-05) * norm_gain + norm_bias


def head_sum(x):
    row, col = iotas(x.shape[-1])
    ones = jnp.where(row // WIDTH == col // WIDTH, 1.0, 0.0)
    return jnp.dot(x, ones, precision=HIGHEST, preferred_element_type=F32)


def prepare(
    acceptor_tokens,
    key_base,
    value_base,
    decay_prod,
    rate_prod,
    blend_prod,
    earliest_block_vals,
    fading_baseline,
    stepsize_baseline,
    residual_blend_baseline,
    erasing_address_factor,
    address_rate_portion,
):
    log_decay = -jnp.exp(-jax.nn.softplus(-(fading_baseline + decay_prod)) - 0.5)
    rate_vals = jax.nn.sigmoid(stepsize_baseline + rate_prod)
    blend_vals = jax.nn.sigmoid(residual_blend_baseline + blend_prod)
    content_tokens = value_base + (earliest_block_vals - value_base) * blend_vals
    removal = key_base * erasing_address_factor
    removal = removal * lax.rsqrt(head_sum(removal * removal) + 1e-06)
    address_signals = key_base * (1.0 + (rate_vals - 1.0) * address_rate_portion)
    return (acceptor_tokens, log_decay, removal, rate_vals, address_signals, content_tokens)


def wrap_around_rule(
    emitted_tokens,
    acceptor_tokens,
    address_signals,
    content_tokens,
    sigmoid_valve_levels,
    present_extra_factor,
    attend_standardize_factor,
    attend_standardize_shift,
):
    centred = emitted_tokens - head_sum(emitted_tokens) * (1.0 / WIDTH)
    head_var = head_sum(centred * centred) * (1.0 / WIDTH)
    per_attend_split = (
        centred * lax.rsqrt(head_var + 0.00064) * attend_standardize_factor
        + attend_standardize_shift
    )
    present_token_extra = (
        head_sum(acceptor_tokens * address_signals * present_extra_factor) * content_tokens
    )
    return (per_attend_split + present_token_extra) * sigmoid_valve_levels


def spread_rows(block_rows):
    return lax.all_gather(block_rows, "head", axis=0, tiled=True)


def collect_rows(partial_value):
    return lax.psum_scatter(
        partial_value.astype(BF16), "head", scatter_dimension=0, tiled=True
    ).astype(F32)


def with_before(token_rows):
    arriving = shifted(token_rows[-1:], "seq", 1)
    return jnp.concatenate([arriving, token_rows[:-1]], axis=0)


def fold_before(grad_rows, grad_before):
    arriving = shifted(grad_before[:1], "seq", -1)
    return grad_rows + jnp.concatenate([grad_before[1:], arriving], axis=0)


def sum_over(part, axis):
    return jnp.sum(lax.all_gather(part, axis, axis=0), axis=0)


def scatter_sum(part, axis):
    count = lax.axis_size(axis)
    pieces = part.astype(BF16).reshape((count, part.shape[0] // count) + part.shape[1:])
    pieces = lax.all_to_all(pieces, axis, split_axis=0, concat_axis=0)
    return jnp.sum(pieces.astype(F32), axis=0)


def columns(whole, widths):
    pieces, at = [], 0
    for width in widths:
        pieces.append(whole[:, at : at + width])
        at += width
    return pieces


def body(
    incoming_hidden,
    earliest_block_vals,
    upstream_sensitivity,
    opening_standardize_factor,
    opening_standardize_shift,
    attention_lag_blend,
    acceptor_linear_map,
    address_linear_map,
    content_linear_map,
    fading_narrowing,
    fading_widening,
    fading_baseline,
    stepsize_narrowing,
    stepsize_widening,
    stepsize_baseline,
    residual_blend_narrowing,
    residual_blend_widening,
    residual_blend_baseline,
    valve_narrowing,
    valve_widening,
    erasing_address_factor,
    address_rate_portion,
    present_extra_factor,
    attend_standardize_factor,
    attend_standardize_shift,
    emitted_linear_map,
    closing_standardize_factor,
    closing_standardize_shift,
    feedforward_lag_blend,
    feedforward_entrance,
    feedforward_exit,
):
    position = lax.axis_index("seq").astype(jnp.int32).reshape(1)
    early = [
        acceptor_linear_map,
        address_linear_map,
        content_linear_map,
        fading_narrowing,
        stepsize_narrowing,
        residual_blend_narrowing,
        valve_narrowing,
    ]
    early_widths = [part.shape[1] for part in early]
    wideners = [fading_widening, stepsize_widening, residual_blend_widening, valve_widening]
    widener_rows = [part.shape[0] for part in wideners]
    late = [emitted_linear_map.T, feedforward_entrance, feedforward_exit.T]
    late_widths = [part.shape[1] for part in late]
    residual_in = incoming_hidden.astype(F32)
    normed_front, front_back = jax.vjp(
        layer_norm, residual_in, opening_standardize_factor, opening_standardize_shift
    )
    normed = spread_rows(normed_front.astype(BF16))
    early_full = lax.all_gather(jnp.concatenate(early, axis=1), "seq", axis=0, tiled=True)
    (
        full_recept,
        full_key,
        full_value,
        full_decay_down,
        full_rate_down,
        full_blend_down,
        full_gate_down,
    ) = columns(early_full, early_widths)
    wide_full = lax.all_gather(jnp.concatenate(wideners, axis=0), "seq", axis=0)
    ups, at = [], 0
    for count in widener_rows:
        ups.append(wide_full[:, at : at + count].reshape(-1, wide_full.shape[-1]))
        at += count
    full_decay_up, full_rate_up, full_blend_up, full_gate_up = ups
    late_full = lax.all_gather(jnp.concatenate(late, axis=1), "seq", axis=0, tiled=True)
    full_output_t, full_channel_key, full_channel_value_t = columns(late_full, late_widths)
    grad_top = spread_rows(upstream_sensitivity)

    normed_wide = normed.astype(F32)
    shift_delta = with_before(normed).astype(F32) - normed_wide
    mixed_in = [
        (normed_wide + shift_delta * attention_lag_blend[p][None]).astype(BF16) for p in range(6)
    ]
    acceptor_tokens = product(mixed_in[0], full_recept)
    key_base = product(mixed_in[2], full_key)
    value_base = product(mixed_in[3], full_value)
    decay_lat = product(mixed_in[1], full_decay_down)
    decay_tanh = jnp.tanh(decay_lat).astype(BF16)
    rate_lat = product(mixed_in[4], full_rate_down).astype(BF16)
    blend_lat = product(mixed_in[3], full_blend_down).astype(BF16)
    gate_pre = product(mixed_in[5], full_gate_down)
    gate_lat = jax.nn.sigmoid(gate_pre).astype(BF16)
    decay_prod = product(decay_tanh, full_decay_up)
    rate_prod = product(rate_lat, full_rate_up)
    blend_prod = product(blend_lat, full_blend_up)
    sigmoid_valve_levels = product(gate_lat, full_gate_up)
    scan_operands, prepare_back = jax.vjp(
        prepare,
        acceptor_tokens,
        key_base,
        value_base,
        decay_prod,
        rate_prod,
        blend_prod,
        earliest_block_vals.astype(F32),
        fading_baseline,
        stepsize_baseline,
        residual_blend_baseline,
        erasing_address_factor,
        address_rate_portion,
    )
    query_map, local_out, saved, ending = core_forward(*scan_operands)
    gathered = lax.all_gather(ending.astype(BF16), "seq", axis=0)
    emitted_tokens, entering = combine(position, gathered, query_map, local_out)
    branch_wide, finish_back = jax.vjp(
        wrap_around_rule,
        emitted_tokens,
        scan_operands[0],
        scan_operands[4],
        scan_operands[5],
        sigmoid_valve_levels,
        present_extra_factor,
        attend_standardize_factor,
        attend_standardize_shift,
    )
    auxiliary_path = branch_wide.astype(BF16)
    middle = residual_in + collect_rows(cross_cols(auxiliary_path, full_output_t))
    normed_mid_front, middle_back = jax.vjp(
        layer_norm, middle, closing_standardize_factor, closing_standardize_shift
    )
    normed_mid = spread_rows(normed_mid_front.astype(BF16))
    mid_wide = normed_mid.astype(F32)
    mid_delta = with_before(normed_mid).astype(F32) - mid_wide
    keyed_in = (mid_wide + mid_delta * feedforward_lag_blend).astype(BF16)
    hidden_pre = product(keyed_in, full_channel_key)
    hidden = jnp.square(jax.nn.relu(hidden_pre)).astype(BF16)
    grad_pre = (product(grad_top, full_channel_value_t) * 2.0 * jax.nn.relu(hidden_pre)).astype(
        BF16
    )
    grad_keyed = cross_cols(grad_pre, full_channel_key)
    feedforward_lag_blend_adjoint = jnp.sum(grad_keyed * mid_delta, axis=0)
    grad_mid_rows = fold_before(
        grad_keyed * (1.0 - feedforward_lag_blend), grad_keyed * feedforward_lag_blend
    )
    grad_middle_in, closing_standardize_factor_adj, closing_standardize_shift_adj = middle_back(
        collect_rows(grad_mid_rows)
    )
    grad_middle = upstream_sensitivity.astype(F32) + grad_middle_in
    grad_attend = spread_rows(grad_middle.astype(BF16))
    result = middle + collect_rows(cross_cols(hidden, full_channel_value_t))
    late_grads = lax.psum_scatter(
        jnp.concatenate(
            [
                cross_rows(grad_attend, auxiliary_path).astype(BF16),
                cross_rows(keyed_in, grad_pre).astype(BF16),
                cross_rows(grad_top, hidden).astype(BF16),
            ],
            axis=1,
        ),
        "seq",
        scatter_dimension=0,
        tiled=True,
    ).astype(F32)
    emitted_t, feedforward_entrance_adjoint, exit_t = columns(late_grads, late_widths)
    emitted_linear_map_adjoint = emitted_t.T
    feedforward_exit_adjoint = exit_t.T
    grad_branch = product(grad_attend, full_output_t)
    (
        grad_outputs,
        grad_recept_extra,
        grad_keys_extra,
        grad_values_extra,
        grad_gate_vals,
        present_extra_adjoint,
        attend_standardize_factor_adj,
        attend_standardize_shift_adj,
    ) = finish_back(grad_branch)
    row, col = iotas(PAIR)
    same_head = (row // WIDTH) == (col // WIDTH)
    grad_local = []
    for p in range(query_map.shape[1] // PAIR):
        lanes = slice(PAIR * p, PAIR * p + PAIR)
        square = lax.dot_general(
            grad_outputs[:, lanes],
            query_map[:, lanes],
            TN,
            precision=HIGHEST,
            preferred_element_type=F32,
        )
        grad_local.append(join_pair(jnp.where(same_head, square, 0.0)))
    grads = lax.all_gather(jnp.stack(grad_local).astype(BF16), "seq", axis=0)
    grad_kernel = core_backward(
        position, gathered, grads, scan_operands, grad_outputs, saved, entering
    )
    grad_kernel = (
        grad_kernel[0] + grad_recept_extra,
        grad_kernel[1],
        grad_kernel[2],
        grad_kernel[3],
        grad_kernel[4] + grad_keys_extra,
        grad_kernel[5] + grad_values_extra,
    )
    (
        grad_recept,
        grad_key_base,
        grad_value_base,
        grad_decay_prod,
        grad_rate_prod,
        grad_blend_prod,
        earliest_block_vals_adjoint,
        fading_baseline_adjoint,
        stepsize_baseline_adjoint,
        residual_blend_baseline_adj,
        erasing_address_factor_adj,
        address_rate_portion_adjoint,
    ) = prepare_back(grad_kernel)
    recept_back = grad_recept.astype(BF16)
    key_back = grad_key_base.astype(BF16)
    value_back = grad_value_base.astype(BF16)
    decay_prod_back = grad_decay_prod.astype(BF16)
    rate_prod_back = grad_rate_prod.astype(BF16)
    blend_prod_back = grad_blend_prod.astype(BF16)
    gate_back = grad_gate_vals.astype(BF16)
    tanh_wide = jnp.tanh(decay_lat)
    gate_sigmoid = jax.nn.sigmoid(gate_pre)
    decay_lat_back = (
        cross_cols(decay_prod_back, full_decay_up) * (1.0 - tanh_wide * tanh_wide)
    ).astype(BF16)
    rate_lat_back = cross_cols(rate_prod_back, full_rate_up).astype(BF16)
    blend_lat_back = cross_cols(blend_prod_back, full_blend_up).astype(BF16)
    gate_pre_back = (
        cross_cols(gate_back, full_gate_up) * gate_sigmoid * (1.0 - gate_sigmoid)
    ).astype(BF16)
    grad_mixed = [
        cross_cols(recept_back, full_recept),
        cross_cols(decay_lat_back, full_decay_down),
        cross_cols(key_back, full_key),
        cross_cols(value_back, full_value) + cross_cols(blend_lat_back, full_blend_down),
        cross_cols(rate_lat_back, full_rate_down),
        cross_cols(gate_pre_back, full_gate_down),
    ]
    shift_sums = jnp.stack([jnp.sum(g * shift_delta, axis=0) for g in grad_mixed])
    plain = sum(grad_mixed)
    lagged = sum(g * attention_lag_blend[p][None] for p, g in enumerate(grad_mixed))
    grad_normed = fold_before(plain - lagged, lagged)
    grad_front_in, opening_standardize_factor_adj, opening_standardize_shift_adj = front_back(
        collect_rows(grad_normed)
    )
    incoming_hidden_adjoint = grad_middle + grad_front_in
    early_grads = scatter_sum(
        jnp.concatenate(
            [
                cross_rows(mixed_in[0], recept_back).astype(BF16),
                cross_rows(mixed_in[2], key_back).astype(BF16),
                cross_rows(mixed_in[3], value_back).astype(BF16),
                cross_rows(mixed_in[1], decay_lat_back).astype(BF16),
                cross_rows(mixed_in[4], rate_lat_back).astype(BF16),
                cross_rows(mixed_in[3], blend_lat_back).astype(BF16),
                cross_rows(mixed_in[5], gate_pre_back).astype(BF16),
            ],
            axis=1,
        ),
        "seq",
    )
    (
        acceptor_linear_map_adjoint,
        address_linear_map_adjoint,
        content_linear_map_adjoint,
    ) = columns(early_grads, early_widths[:3])
    narrow = early_grads[:, sum(early_widths[:3]) :]
    narrow = sum_over(narrow.astype(BF16), "head").astype(F32)
    (
        fading_narrowing_adjoint,
        stepsize_narrowing_adjoint,
        residual_blend_narrowing_adj,
        valve_narrowing_adjoint,
    ) = columns(narrow, early_widths[3:])
    count = lax.axis_size("seq")
    up_parts = [
        cross_rows(lat, back).astype(BF16).reshape(count, rows, -1)
        for lat, back, rows in zip(
            (decay_tanh, rate_lat, blend_lat, gate_lat),
            (decay_prod_back, rate_prod_back, blend_prod_back, gate_back),
            widener_rows,
        )
    ]
    up_sum = lax.all_to_all(jnp.concatenate(up_parts, axis=1), "seq", split_axis=0, concat_axis=0)
    up_sum = jnp.sum(up_sum.astype(F32), axis=0)
    up_grads, at = [], 0
    for rows in widener_rows:
        up_grads.append(up_sum[at : at + rows])
        at += rows
    (
        fading_widening_adjoint,
        stepsize_widening_adjoint,
        residual_blend_widening_adj,
        valve_widening_adjoint,
    ) = up_grads
    everywhere = jnp.concatenate(
        [
            shift_sums,
            jnp.stack(
                [
                    opening_standardize_factor_adj,
                    opening_standardize_shift_adj,
                    closing_standardize_factor_adj,
                    closing_standardize_shift_adj,
                    feedforward_lag_blend_adjoint,
                ]
            ),
        ],
        axis=0,
    )
    everywhere = sum_over(everywhere, "head")
    head_vectors = jnp.stack(
        [
            fading_baseline_adjoint,
            stepsize_baseline_adjoint,
            residual_blend_baseline_adj,
            erasing_address_factor_adj,
            address_rate_portion_adjoint,
            present_extra_adjoint,
            attend_standardize_factor_adj,
            attend_standardize_shift_adj,
        ]
    )
    vectors = sum_over(jnp.concatenate([everywhere.reshape(-1), head_vectors.reshape(-1)]), "seq")
    split = everywhere.size
    everywhere = vectors[:split].reshape(everywhere.shape)
    head_vectors = vectors[split:].reshape(head_vectors.shape)
    shift_sums = everywhere[:6]
    return (
        result.astype(BF16),
        incoming_hidden_adjoint,
        earliest_block_vals_adjoint,
        everywhere[6],
        everywhere[7],
        jnp.concatenate([shift_sums[:1], shift_sums[2:]], axis=0),
        shift_sums[1],
        acceptor_linear_map_adjoint,
        address_linear_map_adjoint,
        content_linear_map_adjoint,
        fading_narrowing_adjoint,
        fading_widening_adjoint,
        head_vectors[0],
        stepsize_narrowing_adjoint,
        stepsize_widening_adjoint,
        head_vectors[1],
        residual_blend_narrowing_adj,
        residual_blend_widening_adj,
        head_vectors[2],
        valve_narrowing_adjoint,
        valve_widening_adjoint,
        head_vectors[3],
        head_vectors[4],
        head_vectors[5],
        head_vectors[6],
        head_vectors[7],
        emitted_linear_map_adjoint,
        everywhere[8],
        everywhere[9],
        everywhere[10],
        feedforward_entrance_adjoint,
        feedforward_exit_adjoint,
    )


def solution(mesh):
    in_specs = (
        P(("seq", "head"), None),
        P("seq", "head"),
        P(("seq", "head"), None),
        P(),
        P(),
        P(),
        P("seq", "head"),
        P("seq", "head"),
        P("seq", "head"),
        P("seq", None),
        P("seq", "head"),
        P("head"),
        P("seq", None),
        P("seq", "head"),
        P("head"),
        P("seq", None),
        P("seq", "head"),
        P("head"),
        P("seq", None),
        P("seq", "head"),
        P("head"),
        P("head"),
        P("head"),
        P("head"),
        P("head"),
        P("head", "seq"),
        P(),
        P(),
        P(),
        P("seq", "head"),
        P("head", "seq"),
    )
    out_specs = (
        P(("seq", "head"), None),
        P(("seq", "head"), None),
        P("seq", "head"),
        P(),
        P(),
        P(),
        P(),
        P("seq", "head"),
        P("seq", "head"),
        P("seq", "head"),
        P("seq", None),
        P("seq", "head"),
        P("head"),
        P("seq", None),
        P("seq", "head"),
        P("head"),
        P("seq", None),
        P("seq", "head"),
        P("head"),
        P("seq", None),
        P("seq", "head"),
        P("head"),
        P("head"),
        P("head"),
        P("head"),
        P("head"),
        P("head", "seq"),
        P(),
        P(),
        P(),
        P("seq", "head"),
        P("head", "seq"),
    )
    return jax.shard_map(body, mesh=mesh, in_specs=in_specs, out_specs=out_specs, check_vma=False)
```
